32 devices in a mesh: gx: 4 (over z), gy: 8 (over y, x, core).
Axes of the slice: x: 2, y: 2, z: 4, core: 2. Of those that a mesh axis runs over, the one named last changes fastest.
Arguments:
- forcing: float32 [16, 128, 512], P(None, 'gy', 'gx'), may hold values from -6 to 6
- pressure_in: float32 [16, 128, 512], P(None, 'gy', 'gx'), may hold values from -6 to 6
- x_coupling: float32 [16, 128, 512], P(None, 'gy', 'gx'), may hold values from 0.5 to 2000
- y_coupling: float32 [16, 128, 512], P(None, 'gy', 'gx'), may hold values from 0.5 to 2000
- z_coupling: float32 [16, 128, 512], P(None, 'gy', 'gx'), may hold values from 0.05 to 0.5
- damping: float32 [16, 128, 512], P(None, 'gy', 'gx'), may hold values from 0.2 to 2
Outputs:
- pressure: float32 [16, 128, 512], P(None, 'gy', 'gx')
- coarse_residual: float32 [8, 64, 256], P(None, 'gy', 'gx')
- coarse_correction: float32 [8, 64, 256], P(None, 'gy')
The draws below stay inside these ranges and needn't reach their ends.
All inputs are finite; a program needn't handle non-finite values.
Results may differ from the reference program's by a relative error of at most 0.0001.
Values sent between devices are 32-bit elements; how exact they have to be, the bound alone decides.
A program may use at most 128 MiB of HBM per device.

```python
import math
import jax
import jax.numpy as jnp
from jax import lax

NZ = 16
COARSE = 3
NX = 512
NY = 128


def coupling_draw(key, shape, flag_shape):
    base_key, flag_key = jax.random.split(key)
    base = jnp.exp(jax.random.uniform(base_key, shape, jnp.float32, math.log(0.5), math.log(2.0)))
    base = jnp.clip(base, 0.5, 2.0)
    strong = jax.random.uniform(flag_key, flag_shape, jnp.float32) < 0.5
    return base * jnp.where(strong, 1000.0, 1.0)


def draw_x_coupling(key, part):
    return coupling_draw(jax.random.fold_in(key, 11), (NZ, NY, NX), (NZ, NY, 1))


def draw_y_coupling(key, part):
    return coupling_draw(jax.random.fold_in(key, 23), (NZ, NY, NX), (NZ, 1, NX))


def block_scale(key, extent, pieces, smallest, top_value):
    loudness = 1.0
    for position, blocks in pieces:
        steps = jax.random.uniform(jax.random.fold_in(jax.random.fold_in(key, 6), position), (blocks,), jnp.float32, smallest / len(pieces), top_value / len(pieces))
        loudness = loudness * jnp.repeat(jnp.exp(steps), extent[position] // blocks).reshape((-1,) + (1,) * (len(extent) - 1 - position))
    return loudness


def gaussian(key, extent, scale, limit, cuts=(), kind=jnp.bfloat16):
    values = scale * jax.random.normal(key, extent, jnp.float32)
    if cuts:
        values = values * block_scale(key, extent, cuts, -0.22, 0.18)
    return jnp.clip(values, -limit, limit).astype(kind)


def setup_inputs(seed: int = 0) -> dict:
    key_of = jax.random.split(jax.random.key(seed), 7)
    forcing = gaussian(key_of[0], (NZ, NY, NX), 1.0, 6.0, ((1, 8), (2, 4)), jnp.float32)
    pressure_in = gaussian(key_of[1], (NZ, NY, NX), 1.0, 6.0, ((1, 8), (2, 4)), jnp.float32)
    x_coupling = draw_x_coupling(jax.random.fold_in(key_of[6], 71), 0)
    y_coupling = draw_y_coupling(jax.random.fold_in(key_of[6], 71), 0)
    z_coupling = jnp.clip(jnp.exp(math.log(0.5) - 2.3025851 * jax.random.uniform(key_of[4], (NZ, NY, NX), jnp.float32) ** block_scale(key_of[4], (NZ, NY, NX), ((1, 8), (2, 4)), -0.2, 0.2)), 0.05, 0.5)
    damping = jnp.clip(jnp.exp(math.log(2.0) - 2.3025851 * jax.random.uniform(key_of[5], (NZ, NY, NX), jnp.float32) ** block_scale(key_of[5], (NZ, NY, NX), ((1, 8), (2, 4)), -0.2, 0.2)), 0.2, 2.0)
    return {"forcing": forcing, "pressure_in": pressure_in, "x_coupling": x_coupling, "y_coupling": y_coupling, "z_coupling": z_coupling, "damping": damping}


RELAX = 0.8


def shifted(values, offset, axis_dim, filler):
    length = values.shape[axis_dim]
    if offset > 0:
        border = jnp.full_like(lax.slice_in_dim(values, 0, offset, axis=axis_dim), filler)
        return jnp.concatenate([border, lax.slice_in_dim(values, 0, length - offset, axis=axis_dim)], axis=axis_dim)
    amount = -offset
    border = jnp.full_like(lax.slice_in_dim(values, 0, amount, axis=axis_dim), filler)
    return jnp.concatenate([lax.slice_in_dim(values, amount, length, axis=axis_dim), border], axis=axis_dim)


def line_solve(low_band, diagonal, up_band, right_side, axis_dim):
    length = right_side.shape[axis_dim]
    stride = 1
    while stride < length:
        before = shifted(diagonal, stride, axis_dim, 1.0)
        after = shifted(diagonal, -stride, axis_dim, 1.0)
        weight_low = -low_band / before
        weight_up = -up_band / after
        new_diag = diagonal + weight_low * shifted(up_band, stride, axis_dim, 0.0) + weight_up * shifted(low_band, -stride, axis_dim, 0.0)
        new_right = right_side + weight_low * shifted(right_side, stride, axis_dim, 0.0) + weight_up * shifted(right_side, -stride, axis_dim, 0.0)
        low_band = weight_low * shifted(low_band, stride, axis_dim, 0.0)
        up_band = weight_up * shifted(up_band, -stride, axis_dim, 0.0)
        diagonal = new_diag
        right_side = new_right
        stride = stride * 2
    return right_side / diagonal


def top_masked(coupling):
    levels = coupling.shape[0]
    keep = (jnp.arange(levels) < levels - 1)[:, None, None]
    return jnp.where(keep, coupling, jnp.zeros_like(coupling))


def vertical(field, z_low, z_top):
    return z_low * shifted(field, 1, 0, 0.0) + z_top * shifted(field, -1, 0, 0.0)


def restrict(field):
    levels, rows, columns = field.shape
    blocks = field.reshape(levels // 2, 2, rows // 2, 2, columns // 2, 2)
    return jnp.sum(blocks, axis=(1, 3, 5)) * 0.125


def reference(forcing, pressure_in, x_coupling, y_coupling, z_coupling, damping):
    z_top = top_masked(z_coupling)
    z_low = shifted(z_top, 1, 0, 0.0)
    x_left = shifted(x_coupling, 1, 2, 0.0)
    y_left = shifted(y_coupling, 1, 1, 0.0)
    diagonal = x_left + x_coupling + y_left + y_coupling + z_low + z_top + damping
    field = pressure_in
    for repeat in range(2):
        source = forcing + y_left * shifted(field, 1, 1, 0.0) + y_coupling * shifted(field, -1, 1, 0.0) + vertical(field, z_low, z_top)
        field = line_solve(-x_left, diagonal, -x_coupling, source, 2)
        source = forcing + x_left * shifted(field, 1, 2, 0.0) + x_coupling * shifted(field, -1, 2, 0.0) + vertical(field, z_low, z_top)
        field = line_solve(-y_left, diagonal, -y_coupling, source, 1)
    applied = diagonal * field - x_left * shifted(field, 1, 2, 0.0) - x_coupling * shifted(field, -1, 2, 0.0) - y_left * shifted(field, 1, 1, 0.0) - y_coupling * shifted(field, -1, 1, 0.0) - vertical(field, z_low, z_top)
    coarse_residual = restrict(forcing - applied)
    coarse_x = restrict(x_coupling)
    coarse_y = restrict(y_coupling)
    coarse_z = restrict(z_coupling)
    coarse_damp = restrict(damping)
    cz_top = top_masked(coarse_z)
    cz_low = shifted(cz_top, 1, 0, 0.0)
    cx_left = shifted(coarse_x, 1, 2, 0.0)
    cy_left = shifted(coarse_y, 1, 1, 0.0)
    coarse_diag = cx_left + coarse_x + cy_left + coarse_y + cz_low + cz_top + coarse_damp
    correction = RELAX * coarse_residual / coarse_diag
    for repeat in range(COARSE - 1):
        applied_coarse = coarse_diag * correction - cx_left * shifted(correction, 1, 2, 0.0) - coarse_x * shifted(correction, -1, 2, 0.0) - cy_left * shifted(correction, 1, 1, 0.0) - coarse_y * shifted(correction, -1, 1, 0.0) - vertical(correction, cz_low, cz_top)
        correction = correction + RELAX * (coarse_residual - applied_coarse) / coarse_diag
    return (field, coarse_residual, correction)
```

```python
import functools

import jax
import jax.numpy as jnp
from jax import lax
from jax.experimental import pallas as pl
from jax.experimental.pallas import tpu as pltpu
from jax.sharding import PartitionSpec as P

COARSE = 3
RELAX = 0.8
MESH = pl.DeviceIdType.MESH


def up(v, s, fill):
    return jnp.concatenate([jnp.full_like(v[:s], fill), v[:-s]], axis=0)


def down(v, s, fill):
    return jnp.concatenate([v[s:], jnp.full_like(v[:s], fill)], axis=0)


def strides_of(length):
    out, s = [], 1
    while s < length:
        out.append(s)
        s *= 2
    return out


class Comm:
    def __init__(self, send_sems):
        self.sems, self.used, self.pending = send_sems, 0, []

    def send(self, src, dst, recv, dev, cond=None):
        copy = pltpu.make_async_remote_copy(
            src_ref=src, dst_ref=dst, send_sem=self.sems.at[self.used], recv_sem=recv,
            device_id=dev, device_id_type=MESH,
        )
        self.used += 1
        self.pending.append((copy, cond))
        if cond is None:
            copy.start()
        else:
            pl.when(cond)(copy.start)

    def finish(self):
        for copy, cond in self.pending:
            if cond is None:
                copy.wait_send()
            else:
                pl.when(cond)(copy.wait_send)


def await_recv(src, dst, sems, recv, dev, cond=None):
    copy = pltpu.make_async_remote_copy(
        src_ref=src, dst_ref=dst, send_sem=sems.at[0], recv_sem=recv, device_id=dev, device_id_type=MESH
    )
    if cond is None:
        copy.wait_recv()
    else:
        pl.when(cond)(copy.wait_recv)


def interface_factor(n, me, ls, le, rs, re, own, tau, sig, bet, tau2, sig2, dlt, kk):
    beta = jnp.zeros_like(ls[0])
    for d in range(n):
        bet[d] = beta
        w = 1.0 / (1.0 - ls[d] * beta)
        t = le[d] * w
        tau[d] = t
        s = t * beta
        sig[d] = s
        beta = re[d] + s * rs[d]
    delta = jnp.zeros_like(ls[0])
    for d in reversed(range(n)):
        dlt[d] = delta
        w = 1.0 / (1.0 - re[d] * delta)
        t = rs[d] * w
        tau2[d] = t
        s = t * delta
        sig2[d] = s
        delta = ls[d] + s * le[d]
    ls_m, le_m, rs_m, re_m = own
    beta, delta = bet[me], dlt[me]
    a, b = 1.0 - beta * ls_m, 1.0 - delta * re_m
    o1, o2 = beta * rs_m, delta * le_m
    inv = 1.0 / (a * b - o1 * o2)
    kk[0], kk[1], kk[2], kk[3] = b * inv, o1 * inv, a * inv, o2 * inv
    kk[4], kk[5] = beta, delta


def interface_solve(n, me, h_left, h_right, gs, ge, tau, tau2, kk):
    alpha = jnp.zeros_like(gs)
    for d in range(n - 1):
        alpha = jnp.where(d < me, h_left(d) + tau[d] * alpha, alpha)
    gamma = jnp.zeros_like(gs)
    for d in reversed(range(1, n)):
        gamma = jnp.where(d > me, h_right(d) + tau2[d] * gamma, gamma)
    p = alpha + kk[4] * gs
    q = gamma + kk[5] * ge
    return kk[0] * p + kk[1] * q, kk[2] * q + kk[3] * p


def kernel(nx, ny, f_ref, p_ref, x_ref, y_ref, z_ref, d_ref, op_ref, or_ref, oc_ref,
           xl_s, xc_s, yl_s, yc_s, zl_s, zt_s, fo_s, p_s, ri_s, g_s, q_s,
           lx_s, rx_s, wx_s, ly_s, ry_s, wy_s,
           sx0, sy0, hx, hyd, hyu, xb, sxb, ycb, syc, yb, shy,
           xtau, xsig, xbet, xtau2, xsig2, xdlt, xkk,
           ytau, ysig, ybet, ytau2, ysig2, ydlt, ykk,
           pair_s, cown, cbuf, rown, rbuf, corr, flip,
           ssem, s0, sx, syco, sy, sc, sr):
    Y, Z, X = xc_s.shape
    CY, CZ = Y // 2, Z // 2
    gx, gy = lax.axis_index("gx"), lax.axis_index("gy")
    has_w, has_e = gx > 0, gx < nx - 1
    has_n, has_s = gy > 0, gy < ny - 1
    west, east = jnp.maximum(gx - 1, 0), jnp.minimum(gx + 1, nx - 1)
    north, south = jnp.maximum(gy - 1, 0), jnp.minimum(gy + 1, ny - 1)
    x_peers = [lax.rem(gx + o, nx) for o in range(1, nx)]
    y_peers = [lax.rem(gy + o, ny) for o in range(1, ny)]

    barrier = pltpu.get_barrier_semaphore()

    def greet(dev):
        pl.semaphore_signal(barrier, inc=1, device_id=dev, device_id_type=MESH)

    for i in x_peers:
        greet((i, gy))
    for j in y_peers:
        greet((gx, j))

    @pl.when(has_n)
    def _():
        for i in x_peers:
            greet((i, north))

    @pl.when(has_s)
    def _():
        for i in x_peers:
            greet((i, south))

    lane = lax.broadcasted_iota(jnp.int32, (Z, X), 1)
    level = lax.broadcasted_iota(jnp.int32, (Z, X), 0)
    lane3 = lax.broadcasted_iota(jnp.int32, (1, 1, X), 2)

    def rows(ref, j):
        return ref[pl.ds(j, Z, stride=Y), :]

    packed = jnp.zeros((Z, X), jnp.float32)
    for j in range(Y):
        v = rows(x_ref, j)
        xc_s[j] = v
        packed = jnp.where(lane == j, v[:, X - 1:], packed)
        yc_s[j] = rows(y_ref, j)
        zv = jnp.where(level < Z - 1, rows(z_ref, j), 0.0)
        zt_s[j] = zv
        zl_s[j] = pltpu.roll(zv, 1, 0)
        fo_s[j] = rows(f_ref, j)
        p_s[j] = rows(p_ref, j)
    sx0[...] = packed
    sy0[0] = yc_s[Y - 1]
    sy0[1] = p_s[Y - 1]
    sy0[2] = p_s[0]

    @pl.when(jnp.logical_not(has_w))
    def _():
        hx[...] = jnp.zeros_like(hx)

    @pl.when(jnp.logical_not(has_n))
    def _():
        hyd[...] = jnp.zeros_like(hyd)
        for d in range(nx):
            cbuf[d, :, 0:3] = jnp.zeros_like(cbuf[d, :, 0:3])
            rbuf[d, 0:2] = jnp.zeros_like(rbuf[d, 0:2])

    @pl.when(jnp.logical_not(has_s))
    def _():
        hyu[...] = jnp.zeros_like(hyu)
        for d in range(nx):
            cbuf[d, :, 3 + CY:] = jnp.zeros_like(cbuf[d, :, 3 + CY:])
            rbuf[d, 2 + CY:] = jnp.zeros_like(rbuf[d, 2 + CY:])

    both = has_n.astype(jnp.int32) + has_s.astype(jnp.int32)
    pl.semaphore_wait(barrier, (nx - 1) + (ny - 1) + (nx - 1) * both)

    comm = Comm(ssem)
    comm.send(sx0, hx, s0.at[0], (east, gy), has_e)
    comm.send(sy0.at[0:2], hyd, s0.at[1], (gx, south), has_s)
    comm.send(sy0.at[2:3], hyu, s0.at[2], (gx, north), has_n)

    half = X // 2
    off = lax.rem(gx, 2) * half
    ii = lax.broadcasted_iota(jnp.int32, (X, X), 0)
    mm = lax.broadcasted_iota(jnp.int32, (X, X), 1)

    def selection(step, start):
        target = lax.rem((ii + (step + 2)) // 2 - 1 + start + X, X)
        return jnp.where(mm == target, 0.125, 0.0)

    def pairs(field):
        v = field.reshape(CY, 2, Z, X)
        pair_s[...] = (v[:, 0] + v[:, 1]).reshape(CY * Z, X)
        return pair_s[pl.ds(0, CY * CZ, stride=2), :] + pair_s[pl.ds(1, CY * CZ, stride=2), :]

    def mxu(a, b):
        return jnp.dot(a, b, precision=lax.Precision.HIGHEST, preferred_element_type=jnp.float32)

    here, there = selection(0, off), selection(0, half - off)
    sel2 = jnp.concatenate([here, there], axis=0)
    zfull = jnp.stack([rows(z_ref, j) for j in range(Y)])
    damp = jnp.stack([rows(d_ref, j) for j in range(Y)])
    for m, (u, v) in enumerate(((xc_s[...], yc_s[...]), (zfull, damp))):
        both_pairs = jnp.concatenate([pairs(u), pairs(v)], axis=1)
        cown[m] = mxu(both_pairs, sel2).reshape(CY, CZ, X)

    await_recv(sx0, hx, ssem, s0.at[0], (east, gy), has_w)
    await_recv(sy0.at[0:2], hyd, ssem, s0.at[1], (gx, south), has_n)
    await_recv(sy0.at[2:3], hyu, ssem, s0.at[2], (gx, north), has_s)

    xc, yc = xc_s[...], yc_s[...]
    border = jnp.stack([jnp.broadcast_to(hx[:, j:j + 1], (Z, X)) for j in range(Y)])
    xl = jnp.where(lane3 == 0, border, pltpu.roll(xc, 1, 2))
    xl_s[...] = xl
    yl = jnp.concatenate([hyd[0:1], yc[:-1]], axis=0)
    yl_s[...] = yl
    zd = zl_s[...] + zt_s[...] + damp
    xs, ys = xl + xc, yl + yc
    ri = 1.0 / (xs + ys + zd)
    ri_s[...] = ri

    a, c, e = yl * ri, yc * ri, (xs + zd) * ri
    for n, s in enumerate(strides_of(Y)):
        a2, c2 = a * up(a, s, 1.0), c * down(c, s, 1.0)
        e2 = e + a * up(e, s, 0.0) + c * down(e, s, 0.0)
        inv = 1.0 / (a2 + c2 + e2)
        wy_s[n, 0], wy_s[n, 1], wy_s[n, 2] = inv, a * inv, c * inv
        a, c, e = a2 * inv, c2 * inv, e2 * inv
    ly_s[...], ry_s[...] = a, c
    syc[0], syc[1], syc[2], syc[3] = a[0], a[Y - 1], c[0], c[Y - 1]
    ycb[gy] = syc[...]
    for j in y_peers:
        comm.send(syc, ycb.at[gy], syco.at[gy], (gx, j))

    def y_local(r):
        for n, s in enumerate(strides_of(Y)):
            r = wy_s[n, 0] * r + wy_s[n, 1] * up(r, s, 0.0) + wy_s[n, 2] * down(r, s, 0.0)
        return r

    def z_terms(v):
        return zl_s[...] * pltpu.roll(v, 1, 1) + zt_s[...] * pltpu.roll(v, Z - 1, 1)

    def x_source(v, above, below):
        lower = jnp.concatenate([above[None], v[:-1]], axis=0)
        upper = jnp.concatenate([v[1:], below[None]], axis=0)
        return (fo_s[...] + yl_s[...] * lower + yc_s[...] * upper + z_terms(v)) * ri_s[...]

    def pack_edges(into, at, v, start):
        for j in range(Y):
            into = jnp.where(lane == start + j, v[j][:, 0:1], into)
            into = jnp.where(lane == start + Y + j, v[j][:, X - 1:], into)
        return into

    r = x_source(p_s[...], hyd[1], hyu[0])
    xl, xc, ri = xl_s[...], xc_s[...], ri_s[...]
    a, c = xl * ri, xc * ri
    e = (yl_s[...] + yc_s[...] + zd) * ri
    for n, s in enumerate(strides_of(X)):
        low, high = lane3 >= s, lane3 < X - s
        am = jnp.where(low, pltpu.roll(a, s, 2), 1.0)
        em = jnp.where(low, pltpu.roll(e, s, 2), 0.0)
        cp = jnp.where(high, pltpu.roll(c, X - s, 2), 1.0)
        ep = jnp.where(high, pltpu.roll(e, X - s, 2), 0.0)
        a2, c2 = a * am, c * cp
        e2 = e + a * em + c * ep
        inv = 1.0 / (a2 + c2 + e2)
        wa, wc = jnp.where(low, a * inv, 0.0), jnp.where(high, c * inv, 0.0)
        wx_s[n, 0], wx_s[n, 1], wx_s[n, 2] = inv, wa, wc
        r = inv * r + wa * pltpu.roll(r, s, 2) + wc * pltpu.roll(r, X - s, 2)
        a, c, e = a2 * inv, c2 * inv, e2 * inv
    g_s[...], lx_s[...], rx_s[...] = r, a, c

    def x_exchange(m, packed):
        sxb[m] = packed
        xb[m, gx] = packed
        for i in x_peers:
            comm.send(sxb.at[m], xb.at[m, gx], sx.at[m, gx], (i, gy))

    packed = pack_edges(jnp.zeros((Z, X), jnp.float32), 0, r, 0)
    packed = pack_edges(packed, 0, a, 2 * Y)
    packed = pack_edges(packed, 0, c, 4 * Y)
    x_exchange(0, packed)

    for i in x_peers:
        comm.send(cown, cbuf.at[gx, :, 3:3 + CY], sc.at[0, gx], (i, gy))
    for m in range(2):
        cbuf[gx, m, 3:3 + CY] = cown[m]
    for i in [gx] + x_peers:
        comm.send(cown.at[:, CY - 3:], cbuf.at[gx, :, 0:3], sc.at[1, gx], (i, south), has_s)
        comm.send(cown.at[:, 0:2], cbuf.at[gx, :, 3 + CY:], sc.at[2, gx], (i, north), has_n)

    for j in y_peers:
        await_recv(syc, ycb.at[j], ssem, syco.at[j], (gx, j))
    interface_factor(
        ny, gy, *[[ycb[d, m] for d in range(ny)] for m in range(4)], [syc[m] for m in range(4)],
        ytau, ysig, ybet, ytau2, ysig2, ydlt, ykk,
    )

    def slot(v, m):
        return v if m == 0 else pltpu.roll(v, X - m * Y, 1)

    def x_collect(m):
        for i in x_peers:
            await_recv(sxb.at[m], xb.at[m, i], ssem, sx.at[m, i], (i, gy))
        if m == 0:
            coefs = [[slot(xb[0, d], 2 + q) for d in range(nx)] for q in range(4)]
            own = [slot(sxb[0], 2 + q) for q in range(4)]
            interface_factor(nx, gx, *coefs, own, xtau, xsig, xbet, xtau2, xsig2, xdlt, xkk)
        gs = [xb[m, d] for d in range(nx)]
        ge = [slot(v, 1) for v in gs]
        return interface_solve(
            nx, gx, lambda d: ge[d] + xsig[d] * gs[d], lambda d: gs[d] + xsig2[d] * ge[d],
            sxb[m], slot(sxb[m], 1), xtau, xtau2, xkk,
        )

    def spread(v):
        return jnp.stack([jnp.broadcast_to(v[:, j:j + 1], (Z, X)) for j in range(Y)])

    def y_half(m):
        left, right = x_collect(m)
        left, right = spread(left), spread(right)
        v = g_s[...] + lx_s[...] * left + rx_s[...] * right
        q_s[...] = v
        before = jnp.where(lane3 == 0, left, pltpu.roll(v, 1, 2))
        after = jnp.where(lane3 == X - 1, right, pltpu.roll(v, X - 1, 2))
        r = (fo_s[...] + xl_s[...] * before + xc_s[...] * after + z_terms(v)) * ri_s[...]
        r = y_local(r)
        g_s[...] = r
        gs, ge = r[0], r[Y - 1]
        shy[m, 0] = ge + ysig[gy] * gs
        shy[m, 1] = gs + ysig2[gy] * ge
        yb[m, gy] = shy[m, 0]
        for j in y_peers:
            side = jnp.where(j > gy, 0, 1)
            comm.send(shy.at[m, side], yb.at[m, gy], sy.at[m, gy], (gx, j))
        for j in y_peers:
            await_recv(shy.at[m, 0], yb.at[m, j], ssem, sy.at[m, j], (gx, j))
        above, below = interface_solve(
            ny, gy, lambda d: yb[m, d], lambda d: yb[m, d], g_s[0], g_s[Y - 1], ytau, ytau2, ykk
        )
        return g_s[...] + ly_s[...] * above[None] + ry_s[...] * below[None], above, below

    v, above, below = y_half(0)
    r = x_source(v, above, below)
    for n, s in enumerate(strides_of(X)):
        r = wx_s[n, 0] * r + wx_s[n, 1] * pltpu.roll(r, s, 2) + wx_s[n, 2] * pltpu.roll(r, X - s, 2)
    g_s[...] = r
    x_exchange(1, pack_edges(jnp.zeros((Z, X), jnp.float32), 0, r, 0))
    v, above, below = y_half(1)

    change = v - q_s[...]
    stacked = jnp.concatenate(
        [pairs(xc_s[...] * change), pairs(xl_s[...] * change), pairs(z_terms(change))], axis=1
    )
    sel3 = jnp.concatenate([selection(1, off), selection(-1, off), here], axis=0)
    partial = mxu(stacked, sel3).reshape(CY, CZ, X)
    rown[...] = partial
    rbuf[gx, 2:2 + CY] = partial
    for i in x_peers:
        comm.send(rown, rbuf.at[gx, 2:2 + CY], sr.at[0, gx], (i, gy))
    for i in [gx] + x_peers:
        comm.send(rown.at[CY - 2:], rbuf.at[gx, 0:2], sr.at[1, gx], (i, south), has_s)
        comm.send(rown.at[0:2], rbuf.at[gx, 2 + CY:], sr.at[2, gx], (i, north), has_n)
    for j in range(Y):
        op_ref[pl.ds(j, Z, stride=Y), :] = v[j]

    for i in x_peers:
        await_recv(cown, cbuf.at[i, :, 3:3 + CY], ssem, sc.at[0, i], (i, gy))
    for i in [gx] + x_peers:
        await_recv(cown.at[:, CY - 3:], cbuf.at[i, :, 0:3], ssem, sc.at[1, i], (i, south), has_n)
        await_recv(cown.at[:, 0:2], cbuf.at[i, :, 3 + CY:], ssem, sc.at[2, i], (i, north), has_s)

    tiles = nx // 2
    first = lane3 < half
    XX = tiles * X
    wide = lax.broadcasted_iota(jnp.int32, (1, 1, XX), 2)

    def whole(m):
        near = [jnp.where(first, cbuf[2 * t, m], cbuf[2 * t + 1, m]) for t in range(tiles)]
        far = [pltpu.roll(jnp.where(first, cbuf[2 * t + 1, m], cbuf[2 * t, m]), half, 2) for t in range(tiles)]
        return jnp.concatenate(near, axis=2), jnp.concatenate(far, axis=2)

    cx, cy = whole(0)
    cz, cd = whole(1)
    czl = lax.broadcasted_iota(jnp.int32, (1, CZ, 1), 1)
    H = CY + 4
    row = lax.broadcasted_iota(jnp.int32, (H, 1, 1), 0)
    inside = jnp.logical_and(
        jnp.logical_or(row >= 2, has_n), jnp.logical_or(row < 2 + CY, has_s)
    )
    cyl, cy = cy[:H], cy[1:]
    cx, cz, cd = cx[1:], cz[1:], cd[1:]
    cd = jnp.where(inside, cd, 1.0)
    ct = jnp.where(czl < CZ - 1, cz, 0.0)
    cl = pltpu.roll(ct, 1, 1)
    cxl = jnp.where(wide == 0, 0.0, pltpu.roll(cx, 1, 2))
    diag = cxl + cx + cyl + cy + cl + ct + cd
    scale = RELAX / diag

    for i in x_peers:
        await_recv(rown, rbuf.at[i, 2:2 + CY], ssem, sr.at[0, i], (i, gy))
    for i in [gx] + x_peers:
        await_recv(rown.at[CY - 2:], rbuf.at[i, 0:2], ssem, sr.at[1, i], (i, south), has_n)
        await_recv(rown.at[0:2], rbuf.at[i, 2 + CY:], ssem, sr.at[2, i], (i, north), has_s)

    res = []
    for t in range(tiles):
        w = jnp.where(lane3 < X - 1, rbuf[2 * t], 0.0) + jnp.where(lane3 > 0, rbuf[2 * t + 1], 0.0)
        if t > 0:
            w = w + jnp.where(lane3 == 0, rbuf[2 * t - 1], 0.0)
        if t < tiles - 1:
            w = w + jnp.where(lane3 == X - 1, rbuf[2 * t + 2], 0.0)
        res.append(w)
        corr[t] = w[2:2 + CY]
    own = corr[gx // 2]
    own = jnp.where(lax.rem(gx, 2) == 0, own, pltpu.roll(own, half, 2))
    for j in range(CY):
        flip[pl.ds(j, CZ, stride=CY), :] = own[j]
    or_ref[...] = flip[0:CZ * CY, :half]
    res = jnp.concatenate(res, axis=2)
    cor = scale * res
    for repeat in range(COARSE - 1):
        lo, n = 1 + repeat, H - 2 - 2 * repeat
        cut = slice(lo, lo + n)
        mid, above, below = cor[1:-1], cor[:-2], cor[2:]
        applied = (
            diag[cut] * mid
            - cxl[cut] * pltpu.roll(mid, 1, 2)
            - cx[cut] * jnp.where(wide < XX - 1, pltpu.roll(mid, XX - 1, 2), 0.0)
            - cyl[cut] * above
            - cy[cut] * below
            - cl[cut] * pltpu.roll(mid, 1, 1)
            - ct[cut] * pltpu.roll(mid, CZ - 1, 1)
        )
        cor = jnp.where(inside[cut], mid + scale[cut] * (res[cut] - applied), 0.0)
    for j in range(CY):
        for t in range(tiles):
            flip[pl.ds((t + 1) * CZ * CY + j, CZ, stride=CY), :] = cor[j][:, t * X:(t + 1) * X]
    for t in range(tiles):
        oc_ref[:, t * X:(t + 1) * X] = flip[(t + 1) * CZ * CY:(t + 2) * CZ * CY, :]
    comm.finish()


def body(nx, ny, *args):
    Z, Y, X = args[0].shape
    CZ, CY = Z // 2, Y // 2
    flat = [v.reshape(Z * Y, X) for v in args]
    f32 = jnp.float32

    def vm(*shape):
        return pltpu.VMEM(shape, f32)

    block = (Y, Z, X)
    nsx, nsy = len(strides_of(X)), len(strides_of(Y))
    tables_x = [vm(nx, Z, X) for _ in range(6)] + [vm(6, Z, X)]
    tables_y = [vm(ny, Z, X) for _ in range(6)] + [vm(6, Z, X)]
    sends = 3 + (ny - 1) * 3 + (nx - 1) * 4 + nx * 4
    dma = pltpu.SemaphoreType.DMA
    scratch = (
        [vm(*block) for _ in range(11)]
        + [vm(*block), vm(*block), vm(nsx, 3, *block), vm(*block), vm(*block), vm(nsy, 3, *block)]
        + [vm(Z, X), vm(3, Z, X), vm(Z, X), vm(2, Z, X), vm(1, Z, X)]
        + [vm(2, nx, Z, X), vm(2, Z, X), vm(ny, 4, Z, X), vm(4, Z, X), vm(2, ny, Z, X), vm(2, 2, Z, X)]
        + tables_x + tables_y
        + [vm(CY * Z, X), vm(2, CY, CZ, X), vm(nx, 2, CY + 5, CZ, X), vm(CY, CZ, X), vm(nx, CY + 4, CZ, X),
           vm(nx // 2, CY, CZ, X), vm((nx // 2 + 1) * CZ * CY, X)]
        + [dma((sends,)), dma((3,)), dma((2, nx)), dma((ny,)), dma((2, ny)), dma((3, nx)), dma((3, nx))]
    )
    p, r, c = pl.pallas_call(
        functools.partial(kernel, nx, ny),
        out_shape=(
            jax.ShapeDtypeStruct((Z * Y, X), f32),
            jax.ShapeDtypeStruct((CZ * CY, X // 2), f32),
            jax.ShapeDtypeStruct((CZ * CY, nx * X // 2), f32),
        ),
        in_specs=[pl.BlockSpec(memory_space=pltpu.VMEM)] * 6,
        out_specs=[pl.BlockSpec(memory_space=pltpu.VMEM)] * 3,
        scratch_shapes=scratch,
        compiler_params=pltpu.CompilerParams(
            collective_id=0, has_side_effects=True, vmem_limit_bytes=48 * 1024 * 1024
        ),
    )(*flat)
    return p.reshape(Z, Y, X), r.reshape(CZ, CY, X // 2), c.reshape(CZ, CY, nx * X // 2)


def solution(mesh):
    nx, ny = mesh.shape["gx"], mesh.shape["gy"]
    split = P(None, "gy", "gx")
    return jax.shard_map(
        functools.partial(body, nx, ny),
        mesh=mesh,
        in_specs=(split,) * 6,
        out_specs=(split, split, P(None, "gy", None)),
        check_vma=False,
    )
```

```python
import functools

import jax
import jax.numpy as jnp
from jax import lax
from jax.experimental import pallas as pl
from jax.experimental.pallas import tpu as pltpu
from jax.sharding import PartitionSpec as P

COARSE = 3
RELAX = 0.8
MESH = pl.DeviceIdType.MESH


def up(v, s, fill):
    return jnp.concatenate([jnp.full_like(v[:s], fill), v[:-s]], axis=0)


def down(v, s, fill):
    return jnp.concatenate([v[s:], jnp.full_like(v[:s], fill)], axis=0)


def strides_of(length):
    out, s = [], 1
    while s < length:
        out.append(s)
        s *= 2
    return out


class Comm:
    def __init__(self, send_sems):
        self.sems, self.used, self.pending = send_sems, 0, []

    def send(self, src, dst, recv, dev, cond=None):
        copy = pltpu.make_async_remote_copy(
            src_ref=src, dst_ref=dst, send_sem=self.sems.at[self.used], recv_sem=recv,
            device_id=dev, device_id_type=MESH,
        )
        self.used += 1
        self.pending.append((copy, cond))
        if cond is None:
            copy.start()
        else:
            pl.when(cond)(copy.start)

    def finish(self):
        for copy, cond in self.pending:
            if cond is None:
                copy.wait_send()
            else:
                pl.when(cond)(copy.wait_send)


def await_recv(src, dst, sems, recv, dev, cond=None):
    copy = pltpu.make_async_remote_copy(
        src_ref=src, dst_ref=dst, send_sem=sems.at[0], recv_sem=recv, device_id=dev, device_id_type=MESH
    )
    if cond is None:
        copy.wait_recv()
    else:
        pl.when(cond)(copy.wait_recv)


def interface_factor(n, me, ls, le, rs, re, own, tau, sig, bet, tau2, sig2, dlt, kk):
    beta = jnp.zeros_like(ls[0])
    for d in range(n):
        bet[d] = beta
        w = 1.0 / (1.0 - ls[d] * beta)
        t = le[d] * w
        tau[d] = t
        s = t * beta
        sig[d] = s
        beta = re[d] + s * rs[d]
    delta = jnp.zeros_like(ls[0])
    for d in reversed(range(n)):
        dlt[d] = delta
        w = 1.0 / (1.0 - re[d] * delta)
        t = rs[d] * w
        tau2[d] = t
        s = t * delta
        sig2[d] = s
        delta = ls[d] + s * le[d]
    ls_m, le_m, rs_m, re_m = own
    beta, delta = bet[me], dlt[me]
    a, b = 1.0 - beta * ls_m, 1.0 - delta * re_m
    o1, o2 = beta * rs_m, delta * le_m
    inv = 1.0 / (a * b - o1 * o2)
    kk[0], kk[1], kk[2], kk[3] = b * inv, o1 * inv, a * inv, o2 * inv
    kk[4], kk[5] = beta, delta


def interface_solve(n, me, h_left, h_right, gs, ge, tau, tau2, kk):
    alpha = jnp.zeros_like(gs)
    for d in range(n - 1):
        alpha = jnp.where(d < me, h_left(d) + tau[d] * alpha, alpha)
    gamma = jnp.zeros_like(gs)
    for d in reversed(range(1, n)):
        gamma = jnp.where(d > me, h_right(d) + tau2[d] * gamma, gamma)
    p = alpha + kk[4] * gs
    q = gamma + kk[5] * ge
    return kk[0] * p + kk[1] * q, kk[2] * q + kk[3] * p


def kernel(nx, ny, f_hbm, p_hbm, x_hbm, y_hbm, z_hbm, d_hbm, op_ref, or_ref, oc_ref,
           xl_s, xc_s, yl_s, yc_s, zl_s, zt_s, fo_s, p_s, ri_s, g_s, q_s,
           lx_s, rx_s, wx_s, ly_s, ry_s, wy_s,
           sx0, sy0, hx, hyd, hyu, xb, sxb, ycb, syc, yb, shy,
           xtau, xsig, xbet, xtau2, xsig2, xdlt, xkk,
           ytau, ysig, ybet, ytau2, ysig2, ydlt, ykk,
           pair_s, cown, cbuf, rown, rbuf, fown, fbuf, flip,
           ssem, s0, sx, syco, sy, sc, sr, sf, ins, sin):
    Y, Z, X = xc_s.shape
    CY, CZ = Y // 2, Z // 2
    gx, gy = lax.axis_index("gx"), lax.axis_index("gy")
    has_w, has_e = gx > 0, gx < nx - 1
    has_n, has_s = gy > 0, gy < ny - 1
    west, east = jnp.maximum(gx - 1, 0), jnp.minimum(gx + 1, nx - 1)
    north, south = jnp.maximum(gy - 1, 0), jnp.minimum(gy + 1, ny - 1)
    x_peers = [lax.rem(gx + o, nx) for o in range(1, nx)]
    y_peers = [lax.rem(gy + o, ny) for o in range(1, ny)]

    loads = []
    for m, ref in enumerate((x_hbm, y_hbm, p_hbm, z_hbm, d_hbm, f_hbm)):
        loads.append(pltpu.make_async_copy(ref, ins.at[m], sin.at[m]))
        loads[m].start()
    x_ref, y_ref, p_ref, z_ref, d_ref, f_ref = [ins.at[m] for m in range(6)]

    barrier = pltpu.get_barrier_semaphore()

    def greet(dev):
        pl.semaphore_signal(barrier, inc=1, device_id=dev, device_id_type=MESH)

    for i in x_peers:
        greet((i, gy))
    for j in y_peers:
        greet((gx, j))

    corners = [
        (jnp.logical_and(h, v), (i, j)) for h, i in ((has_w, west), (has_e, east)) for v, j in ((has_n, north), (has_s, south))
    ]
    for cond, dev in corners:
        pl.when(cond)(functools.partial(greet, dev))

    lane = lax.broadcasted_iota(jnp.int32, (Z, X), 1)
    level = lax.broadcasted_iota(jnp.int32, (Z, X), 0)
    lane3 = lax.broadcasted_iota(jnp.int32, (1, 1, X), 2)

    def rows(ref, j):
        return ref[pl.ds(j, Z, stride=Y), :]

    packed = jnp.zeros((Z, X), jnp.float32)
    for m in range(3):
        loads[m].wait()
    for j in range(Y):
        v = rows(x_ref, j)
        xc_s[j] = v
        packed = jnp.where(lane == j, v[:, X - 1:], packed)
        yc_s[j] = rows(y_ref, j)
        p_s[j] = rows(p_ref, j)
    for m in range(3, 6):
        loads[m].wait()
    for j in range(Y):
        zv = jnp.where(level < Z - 1, rows(z_ref, j), 0.0)
        zt_s[j] = zv
        zl_s[j] = pltpu.roll(zv, 1, 0)
        fo_s[j] = rows(f_ref, j)
    sx0[...] = packed
    sy0[0] = yc_s[Y - 1]
    sy0[1] = p_s[Y - 1]
    sy0[2] = p_s[0]

    @pl.when(jnp.logical_not(has_w))
    def _():
        hx[...] = jnp.zeros_like(hx)
        cbuf[0] = jnp.zeros_like(cbuf[0])
        rbuf[0] = jnp.zeros_like(rbuf[0])

    @pl.when(jnp.logical_not(has_e))
    def _():
        cbuf[2] = jnp.zeros_like(cbuf[2])
        rbuf[2] = jnp.zeros_like(rbuf[2])

    @pl.when(jnp.logical_not(has_n))
    def _():
        hyd[...] = jnp.zeros_like(hyd)
        for d in range(3):
            cbuf[d, :, 0:3] = jnp.zeros_like(cbuf[d, :, 0:3])
            rbuf[d, 0:2] = jnp.zeros_like(rbuf[d, 0:2])

    @pl.when(jnp.logical_not(has_s))
    def _():
        hyu[...] = jnp.zeros_like(hyu)
        for d in range(3):
            cbuf[d, :, 3 + CY:] = jnp.zeros_like(cbuf[d, :, 3 + CY:])
            rbuf[d, 2 + CY:] = jnp.zeros_like(rbuf[d, 2 + CY:])

    n_corners = sum(cond.astype(jnp.int32) for cond, _ in corners)
    pl.semaphore_wait(barrier, (nx - 1) + (ny - 1) + n_corners)

    comm = Comm(ssem)
    comm.send(sx0, hx, s0.at[0], (east, gy), has_e)
    comm.send(sy0.at[0:2], hyd, s0.at[1], (gx, south), has_s)
    comm.send(sy0.at[2:3], hyu, s0.at[2], (gx, north), has_n)

    half = X // 2
    off = half // 2
    ii = lax.broadcasted_iota(jnp.int32, (X, X), 0)
    mm = lax.broadcasted_iota(jnp.int32, (X, X), 1)

    def selection(step, start):
        target = lax.rem((ii + (step + 2)) // 2 - 1 + start + X, X)
        return jnp.where(mm == target, 0.125, 0.0)

    def pairs(field):
        v = field.reshape(CY, 2, Z, X)
        pair_s[...] = (v[:, 0] + v[:, 1]).reshape(CY * Z, X)
        return pair_s[pl.ds(0, CY * CZ, stride=2), :] + pair_s[pl.ds(1, CY * CZ, stride=2), :]

    def mxu(a, b):
        return jnp.dot(a, b, precision=lax.Precision.HIGHEST, preferred_element_type=jnp.float32)

    here, there = selection(0, off), selection(0, half + off)
    sel2 = jnp.concatenate([here, there], axis=0)
    zfull = jnp.stack([rows(z_ref, j) for j in range(Y)])
    damp = jnp.stack([rows(d_ref, j) for j in range(Y)])
    for m, (u, v) in enumerate(((xc_s[...], yc_s[...]), (zfull, damp))):
        both_pairs = jnp.concatenate([pairs(u), pairs(v)], axis=1)
        cown[m] = mxu(both_pairs, sel2).reshape(CY, CZ, X)

    await_recv(sx0, hx, ssem, s0.at[0], (east, gy), has_w)
    await_recv(sy0.at[0:2], hyd, ssem, s0.at[1], (gx, south), has_n)
    await_recv(sy0.at[2:3], hyu, ssem, s0.at[2], (gx, north), has_s)

    xc, yc = xc_s[...], yc_s[...]
    border = jnp.stack([jnp.broadcast_to(hx[:, j:j + 1], (Z, X)) for j in range(Y)])
    xl = jnp.where(lane3 == 0, border, pltpu.roll(xc, 1, 2))
    xl_s[...] = xl
    yl = jnp.concatenate([hyd[0:1], yc[:-1]], axis=0)
    yl_s[...] = yl
    zd = zl_s[...] + zt_s[...] + damp
    xs, ys = xl + xc, yl + yc
    ri = 1.0 / (xs + ys + zd)
    ri_s[...] = ri

    a, c, e = yl * ri, yc * ri, (xs + zd) * ri
    for n, s in enumerate(strides_of(Y)):
        a2, c2 = a * up(a, s, 1.0), c * down(c, s, 1.0)
        e2 = e + a * up(e, s, 0.0) + c * down(e, s, 0.0)
        inv = 1.0 / (a2 + c2 + e2)
        wy_s[n, 0], wy_s[n, 1], wy_s[n, 2] = inv, a * inv, c * inv
        a, c, e = a2 * inv, c2 * inv, e2 * inv
    ly_s[...], ry_s[...] = a, c
    syc[0], syc[1], syc[2], syc[3] = a[0], a[Y - 1], c[0], c[Y - 1]
    ycb[gy] = syc[...]
    for j in y_peers:
        comm.send(syc, ycb.at[gy], syco.at[gy], (gx, j))

    def y_local(r):
        for n, s in enumerate(strides_of(Y)):
            r = wy_s[n, 0] * r + wy_s[n, 1] * up(r, s, 0.0) + wy_s[n, 2] * down(r, s, 0.0)
        return r

    def z_terms(v):
        return zl_s[...] * pltpu.roll(v, 1, 1) + zt_s[...] * pltpu.roll(v, Z - 1, 1)

    def x_source(v, above, below):
        lower = jnp.concatenate([above[None], v[:-1]], axis=0)
        upper = jnp.concatenate([v[1:], below[None]], axis=0)
        return (fo_s[...] + yl_s[...] * lower + yc_s[...] * upper + z_terms(v)) * ri_s[...]

    def pack_edges(into, at, v, start):
        for j in range(Y):
            into = jnp.where(lane == start + j, v[j][:, 0:1], into)
            into = jnp.where(lane == start + Y + j, v[j][:, X - 1:], into)
        return into

    r = x_source(p_s[...], hyd[1], hyu[0])
    xl, xc, ri = xl_s[...], xc_s[...], ri_s[...]
    a, c = xl * ri, xc * ri
    e = (yl_s[...] + yc_s[...] + zd) * ri
    for n, s in enumerate(strides_of(X)):
        low, high = lane3 >= s, lane3 < X - s
        am = jnp.where(low, pltpu.roll(a, s, 2), 1.0)
        em = jnp.where(low, pltpu.roll(e, s, 2), 0.0)
        cp = jnp.where(high, pltpu.roll(c, X - s, 2), 1.0)
        ep = jnp.where(high, pltpu.roll(e, X - s, 2), 0.0)
        a2, c2 = a * am, c * cp
        e2 = e + a * em + c * ep
        inv = 1.0 / (a2 + c2 + e2)
        wa, wc = jnp.where(low, a * inv, 0.0), jnp.where(high, c * inv, 0.0)
        wx_s[n, 0], wx_s[n, 1], wx_s[n, 2] = inv, wa, wc
        r = inv * r + wa * pltpu.roll(r, s, 2) + wc * pltpu.roll(r, X - s, 2)
        a, c, e = a2 * inv, c2 * inv, e2 * inv
    g_s[...], lx_s[...], rx_s[...] = r, a, c

    def x_exchange(m, packed):
        sxb[m] = packed
        xb[m, gx] = packed
        for i in x_peers:
            comm.send(sxb.at[m], xb.at[m, gx], sx.at[m, gx], (i, gy))

    packed = pack_edges(jnp.zeros((Z, X), jnp.float32), 0, r, 0)
    packed = pack_edges(packed, 0, a, 2 * Y)
    packed = pack_edges(packed, 0, c, 4 * Y)
    x_exchange(0, packed)

    def halo_exchange(src, dst, sems, top, lead, starting):
        def part(ref, lo, n):
            return ref.at[(slice(None),) * lead + (pl.ds(lo, n),)]

        def rows_of(slot):
            return dst.at[slot]

        for slot, i, ok, back in ((0, west, has_w, 2), (1, gx, None, 1), (2, east, has_e, 0)):
            both_ok = (lambda c: c) if ok is None else (lambda c, ok=ok: jnp.logical_and(c, ok))
            if starting:
                if ok is not None:
                    comm.send(src, part(rows_of(back), top, CY), sems.at[0, back], (i, gy), ok)
                comm.send(part(src, CY - top, top), part(rows_of(back), 0, top), sems.at[1, back], (i, south), both_ok(has_s))
                comm.send(part(src, 0, 2), part(rows_of(back), top + CY, 2), sems.at[2, back], (i, north), both_ok(has_n))
            else:
                if ok is not None:
                    await_recv(src, part(rows_of(slot), top, CY), ssem, sems.at[0, slot], (i, gy), ok)
                await_recv(part(src, CY - top, top), part(rows_of(slot), 0, top), ssem, sems.at[1, slot], (i, south), both_ok(has_n))
                await_recv(part(src, 0, 2), part(rows_of(slot), top + CY, 2), ssem, sems.at[2, slot], (i, north), both_ok(has_s))

    for m in range(2):
        cbuf[1, m, 3:3 + CY] = cown[m]
    halo_exchange(cown, cbuf, sc, 3, 1, True)

    for j in y_peers:
        await_recv(syc, ycb.at[j], ssem, syco.at[j], (gx, j))
    interface_factor(
        ny, gy, *[[ycb[d, m] for d in range(ny)] for m in range(4)], [syc[m] for m in range(4)],
        ytau, ysig, ybet, ytau2, ysig2, ydlt, ykk,
    )

    def slot(v, m):
        return v if m == 0 else pltpu.roll(v, X - m * Y, 1)

    def x_collect(m):
        for i in x_peers:
            await_recv(sxb.at[m], xb.at[m, i], ssem, sx.at[m, i], (i, gy))
        if m == 0:
            coefs = [[slot(xb[0, d], 2 + q) for d in range(nx)] for q in range(4)]
            own = [slot(sxb[0], 2 + q) for q in range(4)]
            interface_factor(nx, gx, *coefs, own, xtau, xsig, xbet, xtau2, xsig2, xdlt, xkk)
        gs = [xb[m, d] for d in range(nx)]
        ge = [slot(v, 1) for v in gs]
        return interface_solve(
            nx, gx, lambda d: ge[d] + xsig[d] * gs[d], lambda d: gs[d] + xsig2[d] * ge[d],
            sxb[m], slot(sxb[m], 1), xtau, xtau2, xkk,
        )

    def spread(v):
        return jnp.stack([jnp.broadcast_to(v[:, j:j + 1], (Z, X)) for j in range(Y)])

    def y_half(m):
        left, right = x_collect(m)
        left, right = spread(left), spread(right)
        v = g_s[...] + lx_s[...] * left + rx_s[...] * right
        q_s[...] = v
        before = jnp.where(lane3 == 0, left, pltpu.roll(v, 1, 2))
        after = jnp.where(lane3 == X - 1, right, pltpu.roll(v, X - 1, 2))
        r = (fo_s[...] + xl_s[...] * before + xc_s[...] * after + z_terms(v)) * ri_s[...]
        r = y_local(r)
        g_s[...] = r
        gs, ge = r[0], r[Y - 1]
        shy[m, 0] = ge + ysig[gy] * gs
        shy[m, 1] = gs + ysig2[gy] * ge
        yb[m, gy] = shy[m, 0]
        for j in y_peers:
            side = jnp.where(j > gy, 0, 1)
            comm.send(shy.at[m, side], yb.at[m, gy], sy.at[m, gy], (gx, j))
        for j in y_peers:
            await_recv(shy.at[m, 0], yb.at[m, j], ssem, sy.at[m, j], (gx, j))
        above, below = interface_solve(
            ny, gy, lambda d: yb[m, d], lambda d: yb[m, d], g_s[0], g_s[Y - 1], ytau, ytau2, ykk
        )
        return g_s[...] + ly_s[...] * above[None] + ry_s[...] * below[None], above, below

    v, above, below = y_half(0)
    r = x_source(v, above, below)
    for n, s in enumerate(strides_of(X)):
        r = wx_s[n, 0] * r + wx_s[n, 1] * pltpu.roll(r, s, 2) + wx_s[n, 2] * pltpu.roll(r, X - s, 2)
    g_s[...] = r
    x_exchange(1, pack_edges(jnp.zeros((Z, X), jnp.float32), 0, r, 0))
    v, above, below = y_half(1)

    change = v - q_s[...]
    stacked = jnp.concatenate(
        [pairs(xc_s[...] * change), pairs(xl_s[...] * change), pairs(z_terms(change))], axis=1
    )
    sel3 = jnp.concatenate([selection(1, off), selection(-1, off), here], axis=0)
    partial = mxu(stacked, sel3).reshape(CY, CZ, X)
    rown[...] = partial
    rbuf[1, 2:2 + CY] = partial
    halo_exchange(rown, rbuf, sr, 2, 0, True)
    for j in range(Y):
        op_ref[pl.ds(j, Z, stride=Y), :] = v[j]

    halo_exchange(cown, cbuf, sc, 3, 1, False)

    centre = jnp.logical_and(lane3 >= off, lane3 < off + half)
    wide = lane3

    def planes(m):
        w, o, e = cbuf[0, m], cbuf[1, m], cbuf[2, m]
        near = jnp.where(centre, o, pltpu.roll(jnp.where(lane3 >= half, w, e), half, 2))
        far = jnp.where(centre, pltpu.roll(o, half, 2), jnp.where(lane3 < half, w, e))
        return near, far

    cx, cy = planes(0)
    cz, cd = planes(1)
    czl = lax.broadcasted_iota(jnp.int32, (1, CZ, 1), 1)
    H = CY + 4
    row = lax.broadcasted_iota(jnp.int32, (H, 1, 1), 0)
    inside = jnp.logical_and(
        jnp.logical_or(row >= 2, has_n), jnp.logical_or(row < 2 + CY, has_s)
    )
    inside = jnp.logical_and(
        inside,
        jnp.logical_and(jnp.logical_or(lane3 >= off, has_w), jnp.logical_or(lane3 < off + half, has_e)),
    )
    cyl, cy = cy[:H], cy[1:]
    cx, cz, cd = cx[1:], cz[1:], cd[1:]
    cd = jnp.where(inside, cd, 1.0)
    ct = jnp.where(czl < CZ - 1, cz, 0.0)
    cl = pltpu.roll(ct, 1, 1)
    cxl = pltpu.roll(cx, 1, 2)
    diag = cxl + cx + cyl + cy + cl + ct + cd
    scale = RELAX / diag

    halo_exchange(rown, rbuf, sr, 2, 0, False)
    w, e = pltpu.roll(rbuf[0], half, 2), pltpu.roll(rbuf[2], half, 2)
    res = (
        rbuf[1]
        + jnp.where(jnp.logical_and(lane3 >= off - 2, lane3 <= off), w, 0.0)
        + jnp.where(jnp.logical_and(lane3 >= off + half - 1, lane3 <= off + half + 1), e, 0.0)
    )
    res = jnp.where(inside, res, 0.0)
    cor = scale * res
    for repeat in range(COARSE - 1):
        lo, n = 1 + repeat, H - 2 - 2 * repeat
        cut = slice(lo, lo + n)
        mid, above, below = cor[1:-1], cor[:-2], cor[2:]
        applied = (
            diag[cut] * mid
            - cxl[cut] * pltpu.roll(mid, 1, 2)
            - cx[cut] * pltpu.roll(mid, X - 1, 2)
            - cyl[cut] * above
            - cy[cut] * below
            - cl[cut] * pltpu.roll(mid, 1, 1)
            - ct[cut] * pltpu.roll(mid, CZ - 1, 1)
        )
        cor = jnp.where(inside[cut], mid + scale[cut] * (res[cut] - applied), 0.0)
    hj = CY // 2
    mine = jnp.where(lane3 < half, pltpu.roll(cor[:hj], X - off, 2), pltpu.roll(cor[hj:], off, 2))
    fown[...] = mine
    fbuf[gx] = mine
    for i in x_peers:
        comm.send(fown, fbuf.at[gx], sf.at[gx], (i, gy))
    own = pltpu.roll(res[2:2 + CY], X - off, 2)
    for j in range(CY):
        flip[pl.ds(j, CZ, stride=CY), :] = own[j]
    or_ref[...] = flip[0:CZ * CY, :half]
    for i in x_peers:
        await_recv(fown, fbuf.at[i], ssem, sf.at[i], (i, gy))
    for t in range(nx // 2):
        u, v = fbuf[2 * t], fbuf[2 * t + 1]
        top = jnp.where(lane3 < half, u, pltpu.roll(v, half, 2))
        low = jnp.where(lane3 < half, pltpu.roll(u, half, 2), v)
        base = (t + 1) * CZ * CY
        for j in range(CY):
            flip[pl.ds(base + j, CZ, stride=CY), :] = top[j] if j < hj else low[j - hj]
        oc_ref[:, t * X:(t + 1) * X] = flip[base:base + CZ * CY, :]
    comm.finish()


def put(*refs):
    sems = refs[6]
    copies = [pltpu.make_async_copy(refs[m], refs[3 + m], sems.at[m]) for m in range(3)]
    for copy in copies:
        copy.start()
    for copy in copies:
        copy.wait()


def body(nx, ny, *args):
    Z, Y, X = args[0].shape
    CZ, CY = Z // 2, Y // 2
    flat = [v.reshape(Z * Y, X) for v in args]
    f32 = jnp.float32

    def vm(*shape):
        return pltpu.VMEM(shape, f32)

    block = (Y, Z, X)
    nsx, nsy = len(strides_of(X)), len(strides_of(Y))
    tables_x = [vm(nx, Z, X) for _ in range(6)] + [vm(6, Z, X)]
    tables_y = [vm(ny, Z, X) for _ in range(6)] + [vm(6, Z, X)]
    sends = 3 + (ny - 1) * 3 + (nx - 1) * 3 + 8 * 2
    dma = pltpu.SemaphoreType.DMA
    scratch = (
        [vm(*block) for _ in range(11)]
        + [vm(*block), vm(*block), vm(nsx, 3, *block), vm(*block), vm(*block), vm(nsy, 3, *block)]
        + [vm(Z, X), vm(3, Z, X), vm(Z, X), vm(2, Z, X), vm(1, Z, X)]
        + [vm(2, nx, Z, X), vm(2, Z, X), vm(ny, 4, Z, X), vm(4, Z, X), vm(2, ny, Z, X), vm(2, 2, Z, X)]
        + tables_x + tables_y
        + [vm(CY * Z, X), vm(2, CY, CZ, X), vm(3, 2, CY + 5, CZ, X), vm(CY, CZ, X), vm(3, CY + 4, CZ, X),
           vm(CY // 2, CZ, X), vm(nx, CY // 2, CZ, X), vm((nx // 2 + 1) * CZ * CY, X)]
        + [dma((sends,)), dma((3,)), dma((2, nx)), dma((ny,)), dma((2, ny)), dma((3, 3)), dma((3, 3)), dma((nx,))]
        + [vm(6, Z * Y, X), dma((6,))]
    )
    p, r, c = pl.pallas_call(
        functools.partial(kernel, nx, ny),
        out_shape=(
            jax.ShapeDtypeStruct((Z * Y, X), f32),
            jax.ShapeDtypeStruct((CZ * CY, X // 2), f32),
            jax.ShapeDtypeStruct((CZ * CY, nx * X // 2), f32),
        ),
        in_specs=[pl.BlockSpec(memory_space=pltpu.HBM)] * 6,
        out_specs=[pl.BlockSpec(memory_space=pltpu.VMEM)] * 3,
        scratch_shapes=scratch,
        compiler_params=pltpu.CompilerParams(
            collective_id=0, has_side_effects=True, vmem_limit_bytes=67043328
        ),
    )(*flat)
    return p.reshape(Z, Y, X), r.reshape(CZ, CY, X // 2), c.reshape(CZ, CY, nx * X // 2)


def solution(mesh):
    nx, ny = mesh.shape["gx"], mesh.shape["gy"]
    split = P(None, "gy", "gx")
    return jax.shard_map(
        functools.partial(body, nx, ny),
        mesh=mesh,
        in_specs=(split,) * 6,
        out_specs=(split, split, P(None, "gy", None)),
        check_vma=False,
    )
```

```python
import functools

import jax
import jax.numpy as jnp
from jax import lax
from jax.experimental import pallas as pl
from jax.experimental.pallas import tpu as pltpu
from jax.sharding import PartitionSpec as P

COARSE = 3
RELAX = 0.8
CH = 16
CH2 = 4
MESH = pl.DeviceIdType.MESH


def up(v, s, fill):
    return jnp.concatenate([jnp.full_like(v[:s], fill), v[:-s]], axis=0)


def down(v, s, fill):
    return jnp.concatenate([v[s:], jnp.full_like(v[:s], fill)], axis=0)


def strides_of(length):
    out, s = [], 1
    while s < length:
        out.append(s)
        s *= 2
    return out


class Comm:
    def __init__(self, send_sems):
        self.sems, self.used, self.pending = send_sems, 0, []

    def send(self, src, dst, recv, dev, cond=None):
        copy = pltpu.make_async_remote_copy(
            src_ref=src, dst_ref=dst, send_sem=self.sems.at[self.used], recv_sem=recv,
            device_id=dev, device_id_type=MESH,
        )
        self.used += 1
        self.pending.append((copy, cond))
        if cond is None:
            copy.start()
        else:
            pl.when(cond)(copy.start)

    def finish(self):
        for copy, cond in self.pending:
            if cond is None:
                copy.wait_send()
            else:
                pl.when(cond)(copy.wait_send)


def await_recv(src, dst, sems, recv, dev, cond=None):
    copy = pltpu.make_async_remote_copy(
        src_ref=src, dst_ref=dst, send_sem=sems.at[0], recv_sem=recv, device_id=dev, device_id_type=MESH
    )
    if cond is None:
        copy.wait_recv()
    else:
        pl.when(cond)(copy.wait_recv)


def interface_factor(n, me, ls, le, rs, re, own, tau, sig, bet, tau2, sig2, dlt, kk):
    beta = jnp.zeros_like(ls[0])
    for d in range(n):
        bet[d] = beta
        w = 1.0 / (1.0 - ls[d] * beta)
        t = le[d] * w
        tau[d] = t
        s = t * beta
        sig[d] = s
        beta = re[d] + s * rs[d]
    delta = jnp.zeros_like(ls[0])
    for d in reversed(range(n)):
        dlt[d] = delta
        w = 1.0 / (1.0 - re[d] * delta)
        t = rs[d] * w
        tau2[d] = t
        s = t * delta
        sig2[d] = s
        delta = ls[d] + s * le[d]
    ls_m, le_m, rs_m, re_m = own
    beta, delta = bet[me], dlt[me]
    a, b = 1.0 - beta * ls_m, 1.0 - delta * re_m
    o1, o2 = beta * rs_m, delta * le_m
    inv = 1.0 / (a * b - o1 * o2)
    kk[0], kk[1], kk[2], kk[3] = b * inv, o1 * inv, a * inv, o2 * inv
    kk[4], kk[5] = beta, delta


def interface_solve(n, me, h_left, h_right, gs, ge, tau, tau2, kk):
    alpha = jnp.zeros_like(gs)
    for d in range(n - 1):
        alpha = jnp.where(d < me, h_left(d) + tau[d] * alpha, alpha)
    gamma = jnp.zeros_like(gs)
    for d in reversed(range(1, n)):
        gamma = jnp.where(d > me, h_right(d) + tau2[d] * gamma, gamma)
    p = alpha + kk[4] * gs
    q = gamma + kk[5] * ge
    return kk[0] * p + kk[1] * q, kk[2] * q + kk[3] * p


def kernel(nx, ny, f_hbm, p_hbm, x_hbm, y_hbm, z_hbm, d_hbm, op_hbm, or_hbm, oc_hbm,
           xl_s, xc_s, yl_s, yc_s, zl_s, zt_s, fo_s, p_s, ri_s, g_s, q_s, zds_s,
           lx_s, rx_s, wx_s, ly_s, ry_s, wy_s,
           sx0, sy0, hx, hyd, hyu, xb, sxb, ycb, syc, yb, shy,
           xtau, xsig, xbet, xtau2, xsig2, xdlt, xkk,
           ytau, ysig, ybet, ytau2, ysig2, ydlt, ykk,
           pair_s, cown, cbuf, rown, rbuf, fown, fbuf, flip,
           ssem, s0, sx, syco, sy, sc, sr, sf, ins, sin, op_ref, or_ref, oc_ref, sout):
    Y, Z, X = xc_s.shape
    CY, CZ = Y // 2, Z // 2
    gx, gy = lax.axis_index("gx"), lax.axis_index("gy")
    has_w, has_e = gx > 0, gx < nx - 1
    has_n, has_s = gy > 0, gy < ny - 1
    west, east = jnp.maximum(gx - 1, 0), jnp.minimum(gx + 1, nx - 1)
    north, south = jnp.maximum(gy - 1, 0), jnp.minimum(gy + 1, ny - 1)
    x_peers = [lax.rem(gx + o, nx) for o in range(1, nx)]
    y_peers = [lax.rem(gy + o, ny) for o in range(1, ny)]

    loads = []
    for m, ref in enumerate((x_hbm, y_hbm, p_hbm, z_hbm, d_hbm, f_hbm)):
        loads.append(pltpu.make_async_copy(ref, ins.at[m], sin.at[m]))
        loads[m].start()
    x_ref, y_ref, p_ref, z_ref, d_ref, f_ref = [ins.at[m] for m in range(6)]

    barrier = pltpu.get_barrier_semaphore()

    def greet(dev):
        pl.semaphore_signal(barrier, inc=1, device_id=dev, device_id_type=MESH)

    for i in x_peers:
        greet((i, gy))
    for j in y_peers:
        greet((gx, j))

    corners = [
        (jnp.logical_and(h, v), (i, j)) for h, i in ((has_w, west), (has_e, east)) for v, j in ((has_n, north), (has_s, south))
    ]
    for cond, dev in corners:
        pl.when(cond)(functools.partial(greet, dev))

    lane = lax.broadcasted_iota(jnp.int32, (Z, X), 1)
    level = lax.broadcasted_iota(jnp.int32, (Z, X), 0)
    lane3 = lax.broadcasted_iota(jnp.int32, (1, 1, X), 2)

    def rows(ref, j):
        return ref[pl.ds(j, Z, stride=Y), :]

    packed = jnp.zeros((Z, X), jnp.float32)
    for m in range(3):
        loads[m].wait()
    for j in range(Y):
        v = rows(x_ref, j)
        xc_s[j] = v
        packed = jnp.where(lane == j, v[:, X - 1:], packed)
        yc_s[j] = rows(y_ref, j)
        p_s[j] = rows(p_ref, j)
    for m in range(3, 6):
        loads[m].wait()
    for j in range(Y):
        zv = jnp.where(level < Z - 1, rows(z_ref, j), 0.0)
        zt_s[j] = zv
        zl_s[j] = pltpu.roll(zv, 1, 0)
        fo_s[j] = rows(f_ref, j)
    sx0[...] = packed
    sy0[0] = yc_s[Y - 1]
    sy0[1] = p_s[Y - 1]
    sy0[2] = p_s[0]

    @pl.when(jnp.logical_not(has_w))
    def _():
        hx[...] = jnp.zeros_like(hx)
        cbuf[0] = jnp.zeros_like(cbuf[0])
        rbuf[0] = jnp.zeros_like(rbuf[0])

    @pl.when(jnp.logical_not(has_e))
    def _():
        cbuf[2] = jnp.zeros_like(cbuf[2])
        rbuf[2] = jnp.zeros_like(rbuf[2])

    @pl.when(jnp.logical_not(has_n))
    def _():
        hyd[...] = jnp.zeros_like(hyd)
        for d in range(3):
            cbuf[d, :, 0:3] = jnp.zeros_like(cbuf[d, :, 0:3])
            rbuf[d, 0:2] = jnp.zeros_like(rbuf[d, 0:2])

    @pl.when(jnp.logical_not(has_s))
    def _():
        hyu[...] = jnp.zeros_like(hyu)
        for d in range(3):
            cbuf[d, :, 3 + CY:] = jnp.zeros_like(cbuf[d, :, 3 + CY:])
            rbuf[d, 2 + CY:] = jnp.zeros_like(rbuf[d, 2 + CY:])

    n_corners = sum(cond.astype(jnp.int32) for cond, _ in corners)
    pl.semaphore_wait(barrier, (nx - 1) + (ny - 1) + n_corners)

    comm = Comm(ssem)
    comm.send(sx0, hx, s0.at[0], (east, gy), has_e)
    comm.send(sy0.at[0:2], hyd, s0.at[1], (gx, south), has_s)
    comm.send(sy0.at[2:3], hyu, s0.at[2], (gx, north), has_n)

    half = X // 2
    off = half // 2
    ii = lax.broadcasted_iota(jnp.int32, (X, X), 0)
    mm = lax.broadcasted_iota(jnp.int32, (X, X), 1)

    def selection(step, start):
        target = lax.rem((ii + (step + 2)) // 2 - 1 + start + X, X)
        return jnp.where(mm == target, 0.125, 0.0)

    def pairs(field):
        v = field.reshape(CY, 2, Z, X)
        pair_s[...] = (v[:, 0] + v[:, 1]).reshape(CY * Z, X)
        return pair_s[pl.ds(0, CY * CZ, stride=2), :] + pair_s[pl.ds(1, CY * CZ, stride=2), :]

    def mxu(a, b):
        return jnp.dot(a, b, precision=lax.Precision.HIGHEST, preferred_element_type=jnp.float32)

    here, there = selection(0, off), selection(0, half + off)
    sel2 = jnp.concatenate([here, there], axis=0)
    zfull = jnp.stack([rows(z_ref, j) for j in range(Y)])
    damp = jnp.stack([rows(d_ref, j) for j in range(Y)])
    for m, (u, v) in enumerate(((xc_s[...], yc_s[...]), (zfull, damp))):
        both_pairs = jnp.concatenate([pairs(u), pairs(v)], axis=1)
        cown[m] = mxu(both_pairs, sel2).reshape(CY, CZ, X)

    await_recv(sx0, hx, ssem, s0.at[0], (east, gy), has_w)
    await_recv(sy0.at[0:2], hyd, ssem, s0.at[1], (gx, south), has_n)
    await_recv(sy0.at[2:3], hyu, ssem, s0.at[2], (gx, north), has_s)

    xc, yc = xc_s[...], yc_s[...]
    border = jnp.stack([jnp.broadcast_to(hx[:, j:j + 1], (Z, X)) for j in range(Y)])
    xl = jnp.where(lane3 == 0, border, pltpu.roll(xc, 1, 2))
    xl_s[...] = xl
    yl = jnp.concatenate([hyd[0:1], yc[:-1]], axis=0)
    yl_s[...] = yl
    zd = zl_s[...] + zt_s[...] + damp
    xs, ys = xl + xc, yl + yc
    ri = 1.0 / (xs + ys + zd)
    ri_s[...] = ri

    a, c, e = yl * ri, yc * ri, (xs + zd) * ri
    for n, s in enumerate(strides_of(Y)):
        a2, c2 = a * up(a, s, 1.0), c * down(c, s, 1.0)
        e2 = e + a * up(e, s, 0.0) + c * down(e, s, 0.0)
        inv = 1.0 / (a2 + c2 + e2)
        wy_s[n, 0], wy_s[n, 1], wy_s[n, 2] = inv, a * inv, c * inv
        a, c, e = a2 * inv, c2 * inv, e2 * inv
    ly_s[...], ry_s[...] = a, c
    syc[0], syc[1], syc[2], syc[3] = a[0], a[Y - 1], c[0], c[Y - 1]
    ycb[gy] = syc[...]
    for j in y_peers:
        comm.send(syc, ycb.at[gy], syco.at[gy], (gx, j))

    def y_local(r):
        for n, s in enumerate(strides_of(Y)):
            r = wy_s[n, 0] * r + wy_s[n, 1] * up(r, s, 0.0) + wy_s[n, 2] * down(r, s, 0.0)
        return r

    def z_terms(v):
        return zl_s[...] * pltpu.roll(v, 1, 1) + zt_s[...] * pltpu.roll(v, Z - 1, 1)

    def x_source(v, above, below):
        lower = jnp.concatenate([above[None], v[:-1]], axis=0)
        upper = jnp.concatenate([v[1:], below[None]], axis=0)
        return (fo_s[...] + yl_s[...] * lower + yc_s[...] * upper + z_terms(v)) * ri_s[...]

    def pack_edges(into, at, v, start):
        for j in range(v.shape[0]):
            into = jnp.where(lane == start + at + j, v[j][:, 0:1], into)
            into = jnp.where(lane == start + at + Y + j, v[j][:, X - 1:], into)
        return into

    ones = jnp.ones((1, 1, X), jnp.float32)
    packed = jnp.zeros((Z, X), jnp.float32)
    zds_s[...] = (yl + yc + zd) * ri
    g_s[...] = x_source(p_s[...], hyd[1], hyu[0])
    for lo in range(0, Y, CH):
        part = slice(lo, lo + CH)
        a, c = xl_s[part] * ri_s[part], xc_s[part] * ri_s[part]
        e, r = zds_s[part], g_s[part]
        for n, s in enumerate(strides_of(X)):
            low, high = lane3 >= s, lane3 < X - s
            a_in, c_in = jnp.where(low, a, 0.0), jnp.where(high, c, 0.0)
            a2 = a * jnp.where(low, pltpu.roll(a, s, 2), ones)
            c2 = c * jnp.where(high, pltpu.roll(c, X - s, 2), ones)
            e2 = e + a_in * pltpu.roll(e, s, 2) + c_in * pltpu.roll(e, X - s, 2)
            inv = 1.0 / (a2 + c2 + e2)
            wa, wc = a_in * inv, c_in * inv
            wx_s[n, 0, part], wx_s[n, 1, part], wx_s[n, 2, part] = inv, wa, wc
            r = inv * r + wa * pltpu.roll(r, s, 2) + wc * pltpu.roll(r, X - s, 2)
            a, c, e = a2 * inv, c2 * inv, e2 * inv
        g_s[part], lx_s[part], rx_s[part] = r, a, c
        for q, v in enumerate((r, a, c)):
            packed = pack_edges(packed, lo, v, 2 * q * Y)

    def x_exchange(m, packed):
        sxb[m] = packed
        xb[m, gx] = packed
        for i in x_peers:
            comm.send(sxb.at[m], xb.at[m, gx], sx.at[m, gx], (i, gy))

    x_exchange(0, packed)

    def halo_exchange(src, dst, sems, top, lead, starting):
        def part(ref, lo, n):
            return ref.at[(slice(None),) * lead + (pl.ds(lo, n),)]

        def rows_of(slot):
            return dst.at[slot]

        for slot, i, ok, back in ((0, west, has_w, 2), (1, gx, None, 1), (2, east, has_e, 0)):
            both_ok = (lambda c: c) if ok is None else (lambda c, ok=ok: jnp.logical_and(c, ok))
            if starting:
                if ok is not None:
                    comm.send(src, part(rows_of(back), top, CY), sems.at[0, back], (i, gy), ok)
                comm.send(part(src, CY - top, top), part(rows_of(back), 0, top), sems.at[1, back], (i, south), both_ok(has_s))
                comm.send(part(src, 0, 2), part(rows_of(back), top + CY, 2), sems.at[2, back], (i, north), both_ok(has_n))
            else:
                if ok is not None:
                    await_recv(src, part(rows_of(slot), top, CY), ssem, sems.at[0, slot], (i, gy), ok)
                await_recv(part(src, CY - top, top), part(rows_of(slot), 0, top), ssem, sems.at[1, slot], (i, south), both_ok(has_n))
                await_recv(part(src, 0, 2), part(rows_of(slot), top + CY, 2), ssem, sems.at[2, slot], (i, north), both_ok(has_s))

    for m in range(2):
        cbuf[1, m, 3:3 + CY] = cown[m]
    halo_exchange(cown, cbuf, sc, 3, 1, True)

    for j in y_peers:
        await_recv(syc, ycb.at[j], ssem, syco.at[j], (gx, j))
    interface_factor(
        ny, gy, *[[ycb[d, m] for d in range(ny)] for m in range(4)], [syc[m] for m in range(4)],
        ytau, ysig, ybet, ytau2, ysig2, ydlt, ykk,
    )

    def slot(v, m):
        return v if m == 0 else pltpu.roll(v, X - m * Y, 1)

    def x_collect(m):
        for i in x_peers:
            await_recv(sxb.at[m], xb.at[m, i], ssem, sx.at[m, i], (i, gy))
        if m == 0:
            coefs = [[slot(xb[0, d], 2 + q) for d in range(nx)] for q in range(4)]
            own = [slot(sxb[0], 2 + q) for q in range(4)]
            interface_factor(nx, gx, *coefs, own, xtau, xsig, xbet, xtau2, xsig2, xdlt, xkk)
        gs = [xb[m, d] for d in range(nx)]
        ge = [slot(v, 1) for v in gs]
        return interface_solve(
            nx, gx, lambda d: ge[d] + xsig[d] * gs[d], lambda d: gs[d] + xsig2[d] * ge[d],
            sxb[m], slot(sxb[m], 1), xtau, xtau2, xkk,
        )

    def spread(v):
        return jnp.stack([jnp.broadcast_to(v[:, j:j + 1], (Z, X)) for j in range(Y)])

    def y_half(m):
        left, right = x_collect(m)
        left, right = spread(left), spread(right)
        v = g_s[...] + lx_s[...] * left + rx_s[...] * right
        q_s[...] = v
        before = jnp.where(lane3 == 0, left, pltpu.roll(v, 1, 2))
        after = jnp.where(lane3 == X - 1, right, pltpu.roll(v, X - 1, 2))
        r = (fo_s[...] + xl_s[...] * before + xc_s[...] * after + z_terms(v)) * ri_s[...]
        r = y_local(r)
        g_s[...] = r
        gs, ge = r[0], r[Y - 1]
        shy[m, 0] = ge + ysig[gy] * gs
        shy[m, 1] = gs + ysig2[gy] * ge
        yb[m, gy] = shy[m, 0]
        for j in y_peers:
            side = jnp.where(j > gy, 0, 1)
            comm.send(shy.at[m, side], yb.at[m, gy], sy.at[m, gy], (gx, j))
        for j in y_peers:
            await_recv(shy.at[m, 0], yb.at[m, j], ssem, sy.at[m, j], (gx, j))
        above, below = interface_solve(
            ny, gy, lambda d: yb[m, d], lambda d: yb[m, d], g_s[0], g_s[Y - 1], ytau, ytau2, ykk
        )
        return g_s[...] + ly_s[...] * above[None] + ry_s[...] * below[None], above, below

    v, above, below = y_half(0)
    g_s[...] = x_source(v, above, below)
    packed = jnp.zeros((Z, X), jnp.float32)
    for lo in range(0, Y, CH2):
        part = slice(lo, lo + CH2)
        r = g_s[part]
        for n, s in enumerate(strides_of(X)):
            r = wx_s[n, 0, part] * r + wx_s[n, 1, part] * pltpu.roll(r, s, 2) + wx_s[n, 2, part] * pltpu.roll(r, X - s, 2)
        g_s[part] = r
        packed = pack_edges(packed, lo, r, 0)
    x_exchange(1, packed)
    v, above, below = y_half(1)

    change = v - q_s[...]
    stacked = jnp.concatenate(
        [pairs(xc_s[...] * change), pairs(xl_s[...] * change), pairs(z_terms(change))], axis=1
    )
    sel3 = jnp.concatenate([selection(1, off), selection(-1, off), here], axis=0)
    partial = mxu(stacked, sel3).reshape(CY, CZ, X)
    rown[...] = partial
    rbuf[1, 2:2 + CY] = partial
    halo_exchange(rown, rbuf, sr, 2, 0, True)
    for j in range(Y):
        op_ref[pl.ds(j, Z, stride=Y), :] = v[j]
    out_p = pltpu.make_async_copy(op_ref, op_hbm, sout.at[0])
    out_p.start()

    halo_exchange(cown, cbuf, sc, 3, 1, False)

    centre = jnp.logical_and(lane3 >= off, lane3 < off + half)
    wide = lane3

    def planes(m):
        w, o, e = cbuf[0, m], cbuf[1, m], cbuf[2, m]
        near = jnp.where(centre, o, pltpu.roll(jnp.where(lane3 >= half, w, e), half, 2))
        far = jnp.where(centre, pltpu.roll(o, half, 2), jnp.where(lane3 < half, w, e))
        return near, far

    cx, cy = planes(0)
    cz, cd = planes(1)
    czl = lax.broadcasted_iota(jnp.int32, (1, CZ, 1), 1)
    H = CY + 4
    row = lax.broadcasted_iota(jnp.int32, (H, 1, 1), 0)
    inside = jnp.logical_and(
        jnp.logical_or(row >= 2, has_n), jnp.logical_or(row < 2 + CY, has_s)
    )
    inside = jnp.logical_and(
        inside,
        jnp.logical_and(jnp.logical_or(lane3 >= off, has_w), jnp.logical_or(lane3 < off + half, has_e)),
    )
    cyl, cy = cy[:H], cy[1:]
    cx, cz, cd = cx[1:], cz[1:], cd[1:]
    cd = jnp.where(inside, cd, 1.0)
    ct = jnp.where(czl < CZ - 1, cz, 0.0)
    cl = pltpu.roll(ct, 1, 1)
    cxl = pltpu.roll(cx, 1, 2)
    diag = cxl + cx + cyl + cy + cl + ct + cd
    scale = RELAX / diag

    halo_exchange(rown, rbuf, sr, 2, 0, False)
    w, e = pltpu.roll(rbuf[0], half, 2), pltpu.roll(rbuf[2], half, 2)
    res = (
        rbuf[1]
        + jnp.where(jnp.logical_and(lane3 >= off - 2, lane3 <= off), w, 0.0)
        + jnp.where(jnp.logical_and(lane3 >= off + half - 1, lane3 <= off + half + 1), e, 0.0)
    )
    res = jnp.where(inside, res, 0.0)
    cor = scale * res
    for repeat in range(COARSE - 1):
        lo, n = 1 + repeat, H - 2 - 2 * repeat
        cut = slice(lo, lo + n)
        mid, above, below = cor[1:-1], cor[:-2], cor[2:]
        applied = (
            diag[cut] * mid
            - cxl[cut] * pltpu.roll(mid, 1, 2)
            - cx[cut] * pltpu.roll(mid, X - 1, 2)
            - cyl[cut] * above
            - cy[cut] * below
            - cl[cut] * pltpu.roll(mid, 1, 1)
            - ct[cut] * pltpu.roll(mid, CZ - 1, 1)
        )
        cor = jnp.where(inside[cut], mid + scale[cut] * (res[cut] - applied), 0.0)
    hj = CY // 2
    mine = jnp.where(lane3 < half, pltpu.roll(cor[:hj], X - off, 2), pltpu.roll(cor[hj:], off, 2))
    fown[...] = mine
    fbuf[gx] = mine
    for i in x_peers:
        comm.send(fown, fbuf.at[gx], sf.at[gx], (i, gy))
    own = pltpu.roll(res[2:2 + CY], X - off, 2)
    for j in range(CY):
        flip[pl.ds(j, CZ, stride=CY), :] = own[j]
    or_ref[...] = flip[0:CZ * CY, :half]
    out_r = pltpu.make_async_copy(or_ref, or_hbm, sout.at[1])
    out_r.start()
    for i in x_peers:
        await_recv(fown, fbuf.at[i], ssem, sf.at[i], (i, gy))
    for t in range(nx // 2):
        u, v = fbuf[2 * t], fbuf[2 * t + 1]
        top = jnp.where(lane3 < half, u, pltpu.roll(v, half, 2))
        low = jnp.where(lane3 < half, pltpu.roll(u, half, 2), v)
        base = (t + 1) * CZ * CY
        for j in range(CY):
            flip[pl.ds(base + j, CZ, stride=CY), :] = top[j] if j < hj else low[j - hj]
        oc_ref[:, t * X:(t + 1) * X] = flip[base:base + CZ * CY, :]
    out_c = pltpu.make_async_copy(oc_ref, oc_hbm, sout.at[2])
    out_c.start()
    comm.finish()
    out_p.wait()
    out_r.wait()
    out_c.wait()


def put(*refs):
    sems = refs[9]
    take = [pltpu.make_async_copy(refs[m], refs[6 + m], sems.at[m]) for m in range(3)]
    give = [pltpu.make_async_copy(refs[6 + m], refs[3 + m], sems.at[3 + m]) for m in range(3)]
    for copy in take:
        copy.start()
    for m in range(3):
        take[m].wait()
        give[m].start()
    for copy in give:
        copy.wait()


def body(nx, ny, *args):
    Z, Y, X = args[0].shape
    CZ, CY = Z // 2, Y // 2
    flat = [v.reshape(Z * Y, X) for v in args]
    f32 = jnp.float32

    def vm(*shape):
        return pltpu.VMEM(shape, f32)

    block = (Y, Z, X)
    nsx, nsy = len(strides_of(X)), len(strides_of(Y))
    tables_x = [vm(nx, Z, X) for _ in range(6)] + [vm(6, Z, X)]
    tables_y = [vm(ny, Z, X) for _ in range(6)] + [vm(6, Z, X)]
    sends = 3 + (ny - 1) * 3 + (nx - 1) * 3 + 8 * 2
    dma = pltpu.SemaphoreType.DMA
    scratch = (
        [vm(*block) for _ in range(12)]
        + [vm(*block), vm(*block), vm(nsx, 3, *block), vm(*block), vm(*block), vm(nsy, 3, *block)]
        + [vm(Z, X), vm(3, Z, X), vm(Z, X), vm(2, Z, X), vm(1, Z, X)]
        + [vm(2, nx, Z, X), vm(2, Z, X), vm(ny, 4, Z, X), vm(4, Z, X), vm(2, ny, Z, X), vm(2, 2, Z, X)]
        + tables_x + tables_y
        + [vm(CY * Z, X), vm(2, CY, CZ, X), vm(3, 2, CY + 5, CZ, X), vm(CY, CZ, X), vm(3, CY + 4, CZ, X),
           vm(CY // 2, CZ, X), vm(nx, CY // 2, CZ, X), vm((nx // 2 + 1) * CZ * CY, X)]
        + [dma((sends,)), dma((3,)), dma((2, nx)), dma((ny,)), dma((2, ny)), dma((3, 3)), dma((3, 3)), dma((nx,))]
        + [vm(6, Z * Y, X), dma((6,))]
        + [vm(Z * Y, X), vm(CZ * CY, X // 2), vm(CZ * CY, nx * X // 2), dma((3,))]
    )
    p, r, c = pl.pallas_call(
        functools.partial(kernel, nx, ny),
        out_shape=(
            jax.ShapeDtypeStruct((Z * Y, X), f32),
            jax.ShapeDtypeStruct((CZ * CY, X // 2), f32),
            jax.ShapeDtypeStruct((CZ * CY, nx * X // 2), f32),
        ),
        in_specs=[pl.BlockSpec(memory_space=pltpu.HBM)] * 6,
        out_specs=[pl.BlockSpec(memory_space=pltpu.HBM)] * 3,
        scratch_shapes=scratch,
        compiler_params=pltpu.CompilerParams(
            collective_id=0, has_side_effects=True, vmem_limit_bytes=67043328
        ),
    )(*flat)
    p, r, c = pl.pallas_call(
        put,
        out_shape=tuple(jax.ShapeDtypeStruct(v.shape, f32) for v in (p, r, c)),
        in_specs=[pl.BlockSpec(memory_space=pltpu.HBM)] * 3,
        out_specs=[pl.BlockSpec(memory_space=pltpu.HBM)] * 3,
        scratch_shapes=[pltpu.VMEM(v.shape, f32) for v in (p, r, c)] + [dma((6,))],
        compiler_params=pltpu.CompilerParams(vmem_limit_bytes=67043328),
    )(p, r, c)
    return p.reshape(Z, Y, X), r.reshape(CZ, CY, X // 2), c.reshape(CZ, CY, nx * X // 2)


def solution(mesh):
    nx, ny = mesh.shape["gx"], mesh.shape["gy"]
    split = P(None, "gy", "gx")
    return jax.shard_map(
        functools.partial(body, nx, ny),
        mesh=mesh,
        in_specs=(split,) * 6,
        out_specs=(split, split, P(None, "gy", None)),
        check_vma=False,
    )
```
